512 devices in a mesh: tm: 16 (over y_lo, z), chan: 32 (over y_hi, x, core).
Axes of the slice: x: 4, y: 8 (y_hi: 4, y_lo: 2; y = y_hi * 2 + y_lo), z: 8, core: 2. Of those that a mesh axis runs over, the one named last changes fastest.
Arguments:
- raw_strain: bfloat16 [512, 256000], P('chan', 'tm'), may hold values from -80 to 80
Outputs:
- whitened: bfloat16 [128, 512, 512], P(None, 'chan', 'tm')
- cross_spectra: float32 [2, 128, 512, 512], P(None, 'tm', 'chan')
The draws below stay inside these ranges and needn't reach their ends.
All inputs are finite; a program needn't handle non-finite values.
Results may differ from the reference program's by a relative error of at most 0.0058.
Values may be sent and summed in bfloat16 or wider, within the bound.
A program may use at most 64 MiB of HBM per device.

```python
import math
import jax
import jax.numpy as jnp
from jax import lax

C_DEV = 16
W_DEV = 16
L = 2000
F = 128
K0 = 8
RM = 250
SMOOTH = 16
HOP = 1000
NWIN = 256
CH = 512
NS = 256000
N_TM = 16
N_CHAN = 32


tone_count = 6


def draw_raw_strain(key, part):
    subkeys = jax.random.split(jax.random.fold_in(key, 7), 8)
    segment = HOP // 4
    segments = NS // segment
    noise_part = jax.random.truncated_normal(subkeys[0], -4.0, 4.0, (CH, NS), jnp.float32)
    envelope = jnp.exp(jax.random.uniform(subkeys[1], (CH, segments, 1), jnp.float32, 0.0, math.log(10.0)))
    shared_field = jax.random.truncated_normal(subkeys[6], -4.0, 4.0, (NS,), jnp.float32)
    shared_gain = jnp.exp(jax.random.uniform(subkeys[7], (CH, 1), jnp.float32, math.log(0.2), math.log(1.0)))
    record = (noise_part.reshape(CH, segments, segment) * envelope).reshape(CH, NS)
    record = record + shared_gain * shared_field[None, :]
    tone_bins = jax.random.randint(subkeys[2], (tone_count,), K0, K0 + F)
    slopes = jax.random.uniform(subkeys[3], (tone_count,), jnp.float32, -0.5, 0.5)
    starts = jax.random.uniform(subkeys[4], (tone_count,), jnp.float32, -math.pi, math.pi)
    gains = jnp.exp(jax.random.uniform(subkeys[5], (CH, tone_count), jnp.float32, math.log(0.005), math.log(0.05)))
    sample = jnp.arange(NS, dtype=jnp.int32)
    channel = jnp.arange(CH, dtype=jnp.float32)
    for tone in range(tone_count):
        turns = (tone_bins[tone] * sample % L).astype(jnp.float32) * jnp.float32(2.0 * math.pi / L)
        tone_phase = starts[tone] + slopes[tone] * channel
        record = record + gains[:, tone:tone + 1] * jnp.cos(turns[None, :] + tone_phase[:, None])
    return record.astype(jnp.bfloat16)


def setup_inputs(seed: int = 0) -> dict:
    arg_keys = jax.random.split(jax.random.key(seed), 2)
    raw_strain = draw_raw_strain(jax.random.fold_in(arg_keys[1], 71), 0)
    return {"raw_strain": raw_strain}


def build_table():
    sample_ids = jnp.arange(L, dtype=jnp.int32)[:, None]
    bin_ids = (K0 + jnp.arange(F, dtype=jnp.int32))[None, :]
    turns = (sample_ids * bin_ids % L).astype(jnp.float32) * jnp.float32(2.0 * math.pi / L)
    return jnp.stack([jnp.cos(turns), -jnp.sin(turns)], axis=1).astype(jnp.bfloat16)

def build_kernel():
    positions = jnp.arange(F, dtype=jnp.float32)
    distance = positions[:, None] - positions[None, :]
    weights = jnp.exp(-distance * distance / jnp.float32(2.0 * SMOOTH * SMOOTH))
    return weights / lax.optimization_barrier(jnp.sum(weights, axis=1, keepdims=True))

def normalize(extended):
    box_width = 2 * RM + 1
    box_sums = lax.reduce_window(jnp.abs(extended), jnp.zeros((), extended.dtype), lax.add, (1, box_width), (1, 1), 'VALID')
    abs_level = box_sums / box_width
    inner = extended[:, RM:extended.shape[1] - RM]
    return (inner / (abs_level + 1e-06)).astype(jnp.bfloat16)

def whiten(frames, dft_table, kernel):
    spectrum = jnp.einsum('cwl,lrf->fcrw', frames.astype(jnp.float32), dft_table.astype(jnp.float32), precision=lax.Precision.HIGHEST)
    energy = spectrum[:, :, 0] * spectrum[:, :, 0] + spectrum[:, :, 1] * spectrum[:, :, 1]
    smoothed = jnp.einsum('gf,fcw->gcw', kernel, energy, precision=lax.Precision.HIGHEST)
    return (spectrum * lax.rsqrt(smoothed + 1e-06)[:, :, None]).astype(jnp.bfloat16)

def reference(raw_strain):
    dft_table = build_table()
    kernel = build_kernel()
    groups = raw_strain.reshape(N_CHAN, C_DEV, NS)

    def one_group(group_raw):
        extended = jnp.pad(group_raw.astype(jnp.float32), ((0, 0), (RM, HOP + RM)))
        normalized = normalize(extended)
        pieces = normalized.reshape(C_DEV, NWIN + 1, HOP)
        frames = jnp.concatenate([pieces[:, :-1], pieces[:, 1:]], axis=2)
        return whiten(frames, dft_table, kernel)
    whitened = lax.map(one_group, groups)
    whitened = jnp.transpose(whitened, (1, 0, 2, 3, 4)).reshape(F, CH, 2, NWIN)
    stored = jnp.transpose(whitened.reshape(F, CH, 2, N_TM, W_DEV), (0, 1, 3, 2, 4)).reshape(F, CH, 2 * NWIN)

    def one_bin(bin_spec):
        joined = bin_spec.reshape(CH, 2 * NWIN)
        flipped = jnp.concatenate([bin_spec[:, 1], -bin_spec[:, 0]], axis=1)
        real_part = jnp.dot(joined, joined.T, preferred_element_type=jnp.float32)
        imag_part = jnp.dot(flipped, joined.T, preferred_element_type=jnp.float32)
        return jnp.stack([real_part, imag_part]) / NWIN
    cross_all = lax.map(one_bin, whitened)
    return (stored, jnp.transpose(cross_all, (1, 0, 2, 3)))
```

```python
import math

import jax
import jax.numpy as jnp
import numpy as np
from jax import lax
from jax.sharding import PartitionSpec as P

L = 2000
F = 128
K0 = 8
RM = 250
SMOOTH = 16
HOP = 1000


def from_behind(x, axis, by):
    count = lax.axis_size(axis)
    pairs = [(i, i + by) for i in range(count) if 0 <= i + by < count]
    return lax.ppermute(x, axis, pairs)


def shifted(block, axis, distance):
    devices = range(lax.axis_size(axis))
    route = [((i - distance) % len(devices), i) for i in devices]
    return lax.ppermute(block, axis, route)


def build_table():
    sample_ids = np.arange(L, dtype=np.int64)[:, None]
    bin_ids = (K0 + np.arange(F, dtype=np.int64))[None, :]
    turns = (sample_ids * bin_ids % L).astype(np.float32) * np.float32(2.0 * math.pi / L)
    table = np.stack([np.cos(turns), -np.sin(turns)], axis=1)
    return jnp.asarray(table.astype(jnp.bfloat16))


def build_kernel():
    positions = jnp.arange(F, dtype=jnp.float32)
    distance = positions[:, None] - positions[None, :]
    weights = jnp.exp(-distance * distance / jnp.float32(2.0 * SMOOTH * SMOOTH))
    return weights / jnp.sum(weights, axis=1, keepdims=True)


def prefix_sums(values):
    rows, length = values.shape
    block_len = 256
    blocks = (length + block_len - 1) // block_len
    padded = jnp.pad(values, ((0, 0), (0, blocks * block_len - length)))
    shaped = padded.reshape(rows, blocks, block_len)
    inner = jnp.cumsum(shaped, axis=2)
    totals = inner[:, :, block_len - 1]
    offsets = jnp.cumsum(totals, axis=1) - totals
    running = (inner + offsets[:, :, None]).reshape(rows, blocks * block_len)[:, :length]
    return jnp.concatenate([jnp.zeros((rows, 1), jnp.float32), running], axis=1)


def normalize(extended):
    box_width = 2 * RM + 1
    length = extended.shape[1]
    count = length - 2 * RM
    running = prefix_sums(jnp.abs(extended))
    box_sums = running[:, box_width : box_width + count] - running[:, :count]
    abs_level = box_sums / box_width
    inner = extended[:, RM : length - RM]
    return (inner / (abs_level + 1e-06)).astype(jnp.bfloat16)


def on_device(raw_strain):
    per_group, samples = raw_strain.shape
    windows = samples // HOP
    lead_rim = from_behind(raw_strain[:, samples - RM :], "tm", 1)
    tail_rim = from_behind(raw_strain[:, : HOP + RM], "tm", -1)
    extended = jnp.concatenate([lead_rim, raw_strain, tail_rim], axis=1).astype(jnp.float32)
    normalized = normalize(extended)
    pieces = normalized.reshape(per_group, windows + 1, HOP)
    frames = jnp.concatenate([pieces[:, :-1], pieces[:, 1:]], axis=2)
    spectrum = jnp.einsum(
        "cwl,lrf->fcrw", frames, build_table(), preferred_element_type=jnp.float32
    )
    energy = spectrum[:, :, 0] * spectrum[:, :, 0] + spectrum[:, :, 1] * spectrum[:, :, 1]
    smoothed = jnp.einsum("gf,fcw->gcw", build_kernel(), energy, precision=lax.Precision.HIGHEST)
    whitened = (spectrum * lax.rsqrt(smoothed + 1e-06)[:, :, None]).astype(jnp.bfloat16)
    stored = whitened.reshape(F, per_group, 2 * windows)
    owned = lax.all_to_all(stored, "tm", split_axis=0, concat_axis=2, tiled=True)
    own_bins, _, lane_depth = owned.shape
    window_total = lane_depth // 2
    time_count = lax.axis_size("tm")
    split_parts = owned.reshape(own_bins, per_group, time_count, 2, windows)
    flipped = jnp.stack([split_parts[:, :, :, 1], -split_parts[:, :, :, 0]], axis=3).reshape(
        own_bins, per_group, lane_depth
    )
    left_side = jnp.concatenate([owned, flipped], axis=1)

    everyone = lax.all_gather(owned, "chan", axis=1, tiled=True)
    product = lax.dot_general(
        left_side, everyone, (((2,), (2,)), ((0,), (0,))), preferred_element_type=jnp.float32
    )
    stacked_sum = (
        jnp.transpose(product.reshape(own_bins, 2, per_group, -1), (1, 0, 2, 3)) / window_total
    )
    return (stored, stacked_sum)


def solution(mesh):
    placed = (P("chan", "tm"),)
    return jax.shard_map(
        on_device,
        mesh=mesh,
        in_specs=placed,
        out_specs=(P(None, "chan", "tm"), P(None, "tm", "chan", None)),
        check_vma=False,
    )
```

```python
import functools
import math

import jax
import jax.numpy as jnp
import numpy as np
from jax import lax
from jax.experimental import pallas as pl
from jax.experimental.pallas import tpu as pltpu
from jax.sharding import PartitionSpec as P

L = 2000
F = 128
K0 = 8
RM = 250
SMOOTH = 16
HOP = 1000
CD = 16
WD = 16
LEAD = 256
TAIL = 1280
NBLK = 67
KP = 1024
Q = 2
MESH = pl.DeviceIdType.MESH


def bin_order():
    return (np.arange(32)[None, :] * 4 + np.arange(4)[:, None]).reshape(-1)


def build_table():
    sample_ids = np.arange(L, dtype=np.int64)[:, None]
    bin_ids = (K0 + np.arange(F, dtype=np.int64))[None, :]
    turns = (sample_ids * bin_ids % L).astype(np.float32) * np.float32(2.0 * math.pi / L)
    both = np.stack([np.cos(turns), -np.sin(turns)], axis=0)
    both = both[:, :, bin_order()].transpose(0, 2, 1).reshape(2 * F, 2, HOP)
    out = np.zeros((2, 2 * F, KP), np.float32)
    out[:, :, :HOP] = both.transpose(1, 0, 2)
    return jnp.asarray(out.astype(jnp.bfloat16))


def build_kernel():
    positions = np.arange(F, dtype=np.float32)
    distance = positions[:, None] - positions[None, :]
    weights = np.exp(-distance * distance / np.float32(2.0 * SMOOTH * SMOOTH))
    weights = weights / np.sum(weights, axis=1, keepdims=True, dtype=np.float32)
    order = bin_order()
    return jnp.asarray(weights[order][:, order].astype(np.float32))


def build_band():
    i = np.arange(3 * 256)[:, None]
    j = np.arange(256)[None, :]
    first = LEAD - RM
    band = (i - j >= first) & (i - j <= first + 2 * RM)
    return jnp.asarray(band.astype(np.float32).astype(jnp.bfloat16))


def build_swap():
    out = np.zeros((256, 256), np.float32)
    for w in range(WD):
        for c in range(CD):
            out[w * CD + c, c * WD + w] = 1.0
    return jnp.asarray(out.astype(jnp.bfloat16))


def front_kernel(raw, lead, tail, table, kern, band, swap, stored, packed, ext, norm, pieces, mid):
    for i in range(62):
        ext[1 + i] = raw[:, 256 * i : 256 * i + 256]
    ext[0] = lead[...]
    ext[63, :, 0:128] = raw[:, 15872:16000]
    ext[63, :, 128:256] = tail[:, 0:128]
    for j in range(4):
        ext[64 + j] = tail[:, 128 + 256 * j : 384 + 256 * j]
    ext[68, :, 0:128] = tail[:, 1152:1280]
    ext[68, :, 128:256] = jnp.zeros((CD, 128), jnp.bfloat16)

    box = jnp.zeros((NBLK * CD, 256), jnp.float32)
    for d in range(3):
        box += jnp.dot(
            jnp.abs(ext[d : d + NBLK]).reshape(NBLK * CD, 256),
            band[256 * d : 256 * d + 256, :],
            preferred_element_type=jnp.float32,
        )
    inner = ext[1 : 1 + NBLK].reshape(NBLK * CD, 256).astype(jnp.float32)
    value = inner / (box * jnp.float32(1.0 / (2 * RM + 1)) + jnp.float32(1e-6))
    for i in range(NBLK):
        norm[:, 256 * i : 256 * i + 256] = value[CD * i : CD * i + CD, :]
    for p in range(WD + 1):
        start = p * HOP // 128 * 128
        off = p * HOP - start
        wide = norm[:, start : start + 1152]
        if off:
            wide = pltpu.roll(wide, 1152 - off, 1)
        pieces[CD * p : CD * p + CD, :] = wide[:, :KP].astype(jnp.bfloat16)

    contract = (((1,), (1,)), ((), ()))
    spec = lax.dot_general(
        table[0], pieces[0 : WD * CD, :], contract, preferred_element_type=jnp.float32
    ) + lax.dot_general(
        table[1], pieces[CD : CD + WD * CD, :], contract, preferred_element_type=jnp.float32
    )
    energy = spec[:F] * spec[:F] + spec[F:] * spec[F:]
    smoothed = jnp.dot(
        kern[...], energy, precision=lax.Precision.HIGHEST, preferred_element_type=jnp.float32
    )
    scale = lax.rsqrt(smoothed + jnp.float32(1e-6))
    white = (spec * jnp.concatenate([scale, scale], axis=0)).astype(jnp.bfloat16)
    turned = jnp.dot(white, swap[...], preferred_element_type=jnp.float32)
    group = lax.broadcasted_iota(jnp.int32, (32, 128), 1) // 16
    for hi in range(2):
        parts = []
        for b in range(4):
            for r in range(2):
                part = turned[r * F + b * 32 : r * F + b * 32 + 32, hi * 128 : hi * 128 + 128]
                slot = 2 * b + r
                parts.append(pltpu.roll(part, 16 * slot, 1) if slot else part)
        for lo in range(8):
            ch = hi * 8 + lo
            line = parts[0]
            for slot in range(1, 8):
                line = jnp.where(group == (lo + slot) % 8, parts[slot], line)
            if lo:
                line = pltpu.roll(line, 128 - 16 * lo, 1)
            mid[pl.ds(ch, 32, stride=CD), :] = line
    everything = mid[...]
    packed[...] = everything.reshape(32, CD, 128).astype(jnp.bfloat16)
    for b in range(4):
        turned_b = pltpu.roll(everything, 128 - 32 * b, 1) if b else everything
        stored[:, b] = turned_b[:, :32].reshape(32, CD, 32).astype(jnp.bfloat16)


def front(raw, lead, tail):
    vm = pl.BlockSpec(memory_space=pltpu.VMEM)
    return pl.pallas_call(
        front_kernel,
        out_shape=(
            jax.ShapeDtypeStruct((32, 4, CD, 32), jnp.bfloat16),
            jax.ShapeDtypeStruct((32, CD, 128), jnp.bfloat16),
        ),
        in_specs=[vm] * 7,
        out_specs=(vm, vm),
        scratch_shapes=[
            pltpu.VMEM((NBLK + 2, CD, 256), jnp.bfloat16),
            pltpu.VMEM((CD, 17280), jnp.float32),
            pltpu.VMEM((CD * (WD + 1), KP), jnp.bfloat16),
            pltpu.VMEM((512, 128), jnp.float32),
        ],
        compiler_params=pltpu.CompilerParams(vmem_limit_bytes=48 * 1024 * 1024),
        name="front",
    )(raw, lead, tail, build_table(), build_kernel(), build_band(), build_swap())


def gather_kernel(packed, out, local_sem, s1, r1, sy, ry, sx, rx, sp, rp):
    t = lax.axis_index("tm")
    c = lax.axis_index("chan")
    h, x, k = c // 8, (c // 2) % 4, c % 2

    def at(dh, dx):
        return ((h + dh) % 4) * 8 + ((x + dx) % 4) * 2 + k

    partner = c + 1 - 2 * k
    barrier = pltpu.get_barrier_semaphore()
    for d in range(1, 16):
        pl.semaphore_signal(barrier, inc=1, device_id=((t + d) % 16, c), device_id_type=MESH)
    for other in (at(1, 0), at(3, 0), at(0, 1), at(0, 3), partner):
        pl.semaphore_signal(barrier, inc=1, device_id=(t, other), device_id_type=MESH)
    pl.semaphore_wait(barrier, 20)

    mine = pltpu.make_async_copy(packed.at[t], out.at[c, :, t], local_sem)
    mine.start()
    first = []
    for d in range(1, 16):
        peer = (t + d) % 16
        copy = pltpu.make_async_remote_copy(
            src_ref=packed.at[peer],
            dst_ref=out.at[c, :, t],
            send_sem=s1.at[d],
            recv_sem=r1.at[d],
            device_id=(peer, c),
            device_id_type=MESH,
        )
        copy.start()
        first.append(copy)
    mine.wait()
    for copy in first:
        copy.wait_recv()

    sent = []

    def send(dh, dx, q, to, send_sem, recv_sem):
        block = at(dh, dx)
        copy = pltpu.make_async_remote_copy(
            src_ref=out.at[block, q],
            dst_ref=out.at[block, q],
            send_sem=send_sem,
            recv_sem=recv_sem,
            device_id=(t, to),
            device_id_type=MESH,
        )
        copy.start()
        sent.append(copy)

    def landed(dh, dx, q, sem):
        block = out.at[at(dh, dx), q]
        pltpu.make_async_copy(block, block, sem).wait()

    def along_x(dh, q):
        send(dh, 0, q, at(0, 1), sx.at[dh, 0, q], rx.at[dh, 2, q])
        send(dh, 0, q, at(0, 3), sx.at[dh, 1, q], rx.at[dh, 0, q])

    def to_partner(dh, dx, q):
        send(dh, dx, q, partner, sp.at[dh, dx, q], rp.at[dh, dx, q])

    def own(q):
        send(0, 0, q, at(1, 0), sy.at[0, q], ry.at[2, q])
        send(0, 0, q, at(3, 0), sy.at[1, q], ry.at[0, q])
        along_x(0, q)
        to_partner(0, 0, q)

    def from_y(dh, q):
        landed(dh, 0, q, ry.at[dh - 1, q])
        if dh == 3 and q == 0:
            send(3, 0, 0, at(1, 0), sy.at[2, 0], ry.at[1, 0])
        if dh == 1 and q == 1:
            send(1, 0, 1, at(3, 0), sy.at[2, 1], ry.at[1, 1])
        along_x(dh, q)
        to_partner(dh, 0, q)

    def from_x(dh, dx, q):
        landed(dh, dx, q, rx.at[dh, dx - 1, q])
        if dx == 3 and q == 0:
            send(dh, 3, 0, at(0, 1), sx.at[dh, 2, 0], rx.at[dh, 1, 0])
        if dx == 1 and q == 1:
            send(dh, 1, 1, at(0, 3), sx.at[dh, 2, 1], rx.at[dh, 1, 1])
        to_partner(dh, dx, q)

    own(0)
    own(1)
    from_x(0, 3, 0)
    from_x(0, 1, 0)
    from_y(3, 0)
    from_y(1, 0)
    from_x(0, 3, 1)
    from_x(0, 1, 1)
    from_y(3, 1)
    from_y(1, 1)
    from_x(0, 2, 0)
    from_x(0, 2, 1)
    for dh in (3, 1):
        from_x(dh, 3, 0)
        from_x(dh, 1, 0)
    from_y(2, 0)
    from_y(2, 1)
    for dh in (3, 1):
        from_x(dh, 3, 1)
        from_x(dh, 1, 1)
    for dh in (3, 1):
        from_x(dh, 2, 0)
        from_x(dh, 2, 1)
    from_x(2, 3, 0)
    from_x(2, 1, 0)
    from_x(2, 3, 1)
    from_x(2, 1, 1)
    from_x(2, 2, 0)
    from_x(2, 2, 1)
    for dh in range(4):
        for dx in range(4):
            for q in range(Q):
                block = out.at[((h + dh) % 4) * 8 + ((x + dx) % 4) * 2 + 1 - k, q]
                pltpu.make_async_copy(block, block, rp.at[dh, dx, q]).wait()
    for copy in first + sent:
        copy.wait_send()


def gather(packed):
    dma = pltpu.SemaphoreType.DMA
    return pl.pallas_call(
        gather_kernel,
        out_shape=jax.ShapeDtypeStruct((32, Q, 16, CD, 128), jnp.bfloat16),
        in_specs=[pl.BlockSpec(memory_space=pl.ANY)],
        out_specs=pl.BlockSpec(memory_space=pl.ANY),
        scratch_shapes=[
            dma(()),
            dma((16,)),
            dma((16,)),
            dma((3, 2)),
            dma((3, 2)),
            dma((4, 3, 2)),
            dma((4, 3, 2)),
            dma((4, 4, 2)),
            dma((4, 4, 2)),
        ],
        compiler_params=pltpu.CompilerParams(collective_id=0, has_side_effects=True),
        name="gather",
    )(packed)


def cross_kernel(mine, everyone, out):
    lane = lax.broadcasted_iota(jnp.int32, (CD, 128), 1)
    flip = (lane // 16) % 2
    total = jnp.zeros((2 * 4 * CD, 512), jnp.float32)
    for pair in range(8):
        lefts, rights = [], []
        for t in (2 * pair, 2 * pair + 1):
            joined = mine[0, 0, t].astype(jnp.float32)
            flipped = jnp.where(flip == 0, pltpu.roll(joined, 112, 1), -pltpu.roll(joined, 16, 1))
            rows = []
            for source in (joined, flipped):
                for b in range(4):
                    rows.append(jnp.where(lane // 32 == b, source, 0.0).astype(jnp.bfloat16))
            lefts.append(jnp.concatenate(rows, axis=0))
            rights.append(everyone[:, 0, t].reshape(512, 128))
        total += lax.dot_general(
            jnp.concatenate(lefts, axis=1),
            jnp.concatenate(rights, axis=1),
            (((1,), (1,)), ((), ())),
            preferred_element_type=jnp.float32,
        )
    out[...] = (total * jnp.float32(1.0 / 256.0)).reshape(2, 4, CD, 512)


def cross(everyone):
    mine = lax.dynamic_slice_in_dim(everyone, lax.axis_index("chan"), 1, 0)
    return pl.pallas_call(
        cross_kernel,
        grid=(Q,),
        out_shape=jax.ShapeDtypeStruct((2, 4 * Q, CD, 512), jnp.float32),
        in_specs=[
            pl.BlockSpec((1, 1, 16, CD, 128), lambda q: (0, q, 0, 0, 0)),
            pl.BlockSpec((32, 1, 16, CD, 128), lambda q: (0, q, 0, 0, 0)),
        ],
        out_specs=pl.BlockSpec((2, 4, CD, 512), lambda q: (0, q, 0, 0)),
        compiler_params=pltpu.CompilerParams(vmem_limit_bytes=40 * 1024 * 1024),
        name="cross",
    )(mine, everyone)


def from_behind(x, axis, by):
    count = lax.axis_size(axis)
    pairs = [(i, i + by) for i in range(count) if 0 <= i + by < count]
    return lax.ppermute(x, axis, pairs)


def on_device(raw):
    samples = raw.shape[1]
    lead = from_behind(raw[:, samples - LEAD :], "tm", 1)
    tail = from_behind(raw[:, :TAIL], "tm", -1)
    stored, packed = front(raw, lead, tail)
    everyone = gather(packed.reshape(16, Q, CD, 128))
    return stored.reshape(F, CD, 2 * WD), cross(everyone)


def solution(mesh):
    return jax.shard_map(
        on_device,
        mesh=mesh,
        in_specs=(P("chan", "tm"),),
        out_specs=(P(None, "chan", "tm"), P(None, "tm", "chan", None)),
        check_vma=False,
    )
```

```python
import math

import jax
import jax.numpy as jnp
import numpy as np
from jax import lax
from jax.experimental import pallas as pl
from jax.experimental.pallas import tpu as pltpu
from jax.sharding import PartitionSpec as P

L = 2000
F = 128
K0 = 8
RM = 250
SMOOTH = 16
HOP = 1000
CD = 16
WD = 16
LEAD = 256
TAIL = 1280
NBLK = 67
KP = 1024
PAIRS = 64
MESH = pl.DeviceIdType.MESH


def bin_order():
    return (np.arange(PAIRS)[None, :] * 2 + np.arange(2)[:, None]).reshape(-1)


def build_table():
    sample_ids = np.arange(L, dtype=np.int64)[:, None]
    bin_ids = (K0 + np.arange(F, dtype=np.int64))[None, :]
    turns = (sample_ids * bin_ids % L).astype(np.float32) * np.float32(2.0 * math.pi / L)
    both = np.stack([np.cos(turns), -np.sin(turns)], axis=0)
    both = both[:, :, bin_order()].transpose(0, 2, 1).reshape(2 * F, 2, HOP)
    out = np.zeros((2, 2 * F, KP), np.float32)
    out[:, :, :HOP] = both.transpose(1, 0, 2)
    return jnp.asarray(out.astype(jnp.bfloat16))


def build_kernel():
    positions = np.arange(F, dtype=np.float32)
    distance = positions[:, None] - positions[None, :]
    weights = np.exp(-distance * distance / np.float32(2.0 * SMOOTH * SMOOTH))
    weights = weights / np.sum(weights, axis=1, keepdims=True, dtype=np.float32)
    order = bin_order()
    return jnp.asarray(weights[order][:, order].astype(np.float32))


def build_band():
    i = np.arange(3 * 256)[:, None]
    j = np.arange(256)[None, :]
    first = LEAD - RM
    band = (i - j >= first) & (i - j <= first + 2 * RM)
    return jnp.asarray(band.astype(np.float32).astype(jnp.bfloat16))


def build_swap():
    out = np.zeros((256, 256), np.float32)
    for w in range(WD):
        for c in range(CD):
            out[w * CD + c, c * WD + w] = 1.0
    return jnp.asarray(out.astype(jnp.bfloat16))


def front_kernel(
    raw_hbm, table_hbm, kern_hbm, band_hbm, swap_hbm, stored, packed,
    raw, lead, tail, table, kern, band, swap, ext, norm, pieces, mid, load_sem, halo_send, halo_recv
):
    t = lax.axis_index("tm")
    c = lax.axis_index("chan")
    loads = []
    for n, (src, dst) in enumerate(
        ((raw_hbm, raw), (band_hbm, band), (table_hbm, table), (kern_hbm, kern), (swap_hbm, swap))
    ):
        load = pltpu.make_async_copy(src, dst, load_sem.at[n])
        load.start()
        loads.append(load)
    after, before = (t + 1) % 16, (t + 15) % 16
    barrier = pltpu.get_barrier_semaphore()
    for other in (after, before):
        pl.semaphore_signal(barrier, inc=1, device_id=(other, c), device_id_type=MESH)
    pl.semaphore_wait(barrier, 2)
    halos = []
    for n, (first, count, dst, other) in enumerate(
        ((raw_hbm.shape[1] - LEAD, LEAD, lead, after), (0, TAIL, tail, before))
    ):
        halo = pltpu.make_async_remote_copy(
            src_ref=raw_hbm.at[:, first : first + count],
            dst_ref=dst,
            send_sem=halo_send.at[n],
            recv_sem=halo_recv.at[n],
            device_id=(other, c),
            device_id_type=MESH,
        )
        halo.start()
        halos.append(halo)
    loads[0].wait()
    for i in range(62):
        ext[1 + i] = raw[:, 256 * i : 256 * i + 256]
    ext[63, :, 0:128] = raw[:, 15872:16000]
    ext[68, :, 128:256] = jnp.zeros((CD, 128), jnp.bfloat16)
    for halo in halos:
        halo.wait_recv()
    has_lead = jnp.full((CD, LEAD), t, jnp.int32) > 0
    has_tail = jnp.full((CD, TAIL), t, jnp.int32) < 15
    ext[0] = jnp.where(has_lead, lead[...].astype(jnp.float32), 0.0).astype(jnp.bfloat16)
    behind = jnp.where(has_tail, tail[...].astype(jnp.float32), 0.0).astype(jnp.bfloat16)
    ext[63, :, 128:256] = behind[:, 0:128]
    for j in range(4):
        ext[64 + j] = behind[:, 128 + 256 * j : 384 + 256 * j]
    ext[68, :, 0:128] = behind[:, 1152:1280]
    for load in loads[1:]:
        load.wait()

    box = jnp.zeros((NBLK * CD, 256), jnp.float32)
    for d in range(3):
        box += jnp.dot(
            jnp.abs(ext[d : d + NBLK]).reshape(NBLK * CD, 256),
            band[256 * d : 256 * d + 256, :],
            preferred_element_type=jnp.float32,
        )
    inner = ext[1 : 1 + NBLK].reshape(NBLK * CD, 256).astype(jnp.float32)
    value = inner / (box * jnp.float32(1.0 / (2 * RM + 1)) + jnp.float32(1e-6))
    for i in range(NBLK):
        norm[:, 256 * i : 256 * i + 256] = value[CD * i : CD * i + CD, :]
    for p in range(WD + 1):
        start = p * HOP // 128 * 128
        off = p * HOP - start
        wide = norm[:, start : start + 1152]
        if off:
            wide = pltpu.roll(wide, 1152 - off, 1)
        pieces[CD * p : CD * p + CD, :] = wide[:, :KP].astype(jnp.bfloat16)

    contract = (((1,), (1,)), ((), ()))
    spec = lax.dot_general(
        table[0], pieces[0 : WD * CD, :], contract, preferred_element_type=jnp.float32
    ) + lax.dot_general(
        table[1], pieces[CD : CD + WD * CD, :], contract, preferred_element_type=jnp.float32
    )
    energy = spec[:F] * spec[:F] + spec[F:] * spec[F:]
    smoothed = jnp.dot(
        kern[...], energy, precision=lax.Precision.HIGHEST, preferred_element_type=jnp.float32
    )
    scale = lax.rsqrt(smoothed + jnp.float32(1e-6))
    white = (spec * jnp.concatenate([scale, scale], axis=0)).astype(jnp.bfloat16)
    turned = jnp.dot(white, swap[...], preferred_element_type=jnp.float32)
    group = lax.broadcasted_iota(jnp.int32, (PAIRS, 128), 1) // 16
    parts = []
    for b in range(2):
        for half in range(2):
            for r in range(2):
                row = r * F + b * PAIRS
                part = turned[row : row + PAIRS, half * 128 : half * 128 + 128]
                slot = len(parts)
                parts.append(pltpu.roll(part, 16 * slot, 1) if slot else part)
    for ih in range(8):
        line = parts[0]
        for slot in range(1, 8):
            line = jnp.where(group == (ih + slot) % 8, parts[slot], line)
        if ih:
            line = pltpu.roll(line, 128 - 16 * ih, 1)
        mid[pl.ds(ih, PAIRS, stride=8), :] = line
    everything = mid[...]
    packed[...] = everything.reshape(PAIRS, 8, 128).astype(jnp.bfloat16)
    for b in range(2):
        halves = []
        for half in range(2):
            by = 64 * b + 32 * half
            turned_b = pltpu.roll(everything, 128 - by, 1) if by else everything
            halves.append(turned_b[:, :32].reshape(PAIRS, 8, 32))
        stored[:, b] = jnp.concatenate(halves, axis=1).astype(jnp.bfloat16)
    for halo in halos:
        halo.wait_send()


def front(raw):
    vm = pl.BlockSpec(memory_space=pltpu.VMEM)
    anywhere = pl.BlockSpec(memory_space=pl.ANY)
    dma = pltpu.SemaphoreType.DMA
    bf16, f32 = jnp.bfloat16, jnp.float32
    return pl.pallas_call(
        front_kernel,
        out_shape=(
            jax.ShapeDtypeStruct((PAIRS, 2, CD, 32), bf16),
            jax.ShapeDtypeStruct((PAIRS, 8, 128), bf16),
        ),
        in_specs=[anywhere] * 5,
        out_specs=(vm, vm),
        scratch_shapes=[
            pltpu.VMEM(raw.shape, bf16),
            pltpu.VMEM((CD, LEAD), bf16),
            pltpu.VMEM((CD, TAIL), bf16),
            pltpu.VMEM((2, 2 * F, KP), bf16),
            pltpu.VMEM((F, F), f32),
            pltpu.VMEM((768, 256), bf16),
            pltpu.VMEM((256, 256), bf16),
            pltpu.VMEM((NBLK + 2, CD, 256), bf16),
            pltpu.VMEM((CD, 17280), f32),
            pltpu.VMEM((CD * (WD + 1), KP), bf16),
            pltpu.VMEM((512, 128), f32),
            dma((5,)),
            dma((2,)),
            dma((2,)),
        ],
        compiler_params=pltpu.CompilerParams(
            vmem_limit_bytes=60 * 1024 * 1024, collective_id=1, has_side_effects=True
        ),
        name="front",
    )(raw, build_table(), build_kernel(), build_band(), build_swap())


def cross_kernel(packed, out, land, flat, both, left, result, own_sem, s1, r1, sy, ry, sp, rp, so, ro):
    t = lax.axis_index("tm")
    c = lax.axis_index("chan")
    h, x, k = c // 8, (c // 2) % 4, c % 2

    def chan(dh, dx):
        return ((h + dh) % 4) * 8 + ((x + dx) % 4) * 2 + k

    partner = c + 1 - 2 * k
    others = [(dt, dx) for dx in range(4) for dt in range(16) if dt or dx]
    barrier = pltpu.get_barrier_semaphore()
    for dt, dx in others:
        pl.semaphore_signal(
            barrier, inc=1, device_id=((t + dt) % 16, chan(0, dx)), device_id_type=MESH
        )
    for other in (chan(1, 0), chan(3, 0), partner):
        pl.semaphore_signal(barrier, inc=1, device_id=(t, other), device_id_type=MESH)
    pl.semaphore_wait(barrier, len(others) + 3)

    place = land.at[t % 2, x, t // 2]
    own = pltpu.make_async_copy(packed.at[t, x], place, own_sem)
    own.start()
    for dt, dx in others:
        to_t, to_x = (t + dt) % 16, (x + dx) % 4
        pltpu.make_async_remote_copy(
            src_ref=packed.at[to_t, to_x],
            dst_ref=place,
            send_sem=s1,
            recv_sem=r1,
            device_id=(to_t, chan(0, dx)),
            device_id_type=MESH,
        ).start()
    own.wait()
    count = flat.at[pl.ds(0, len(others))]
    pltpu.make_async_copy(count, count, r1).wait()

    lane = lax.broadcasted_iota(jnp.int32, (256, 128), 1)
    low = (lane // 32) % 2 == 0
    even = land[0].astype(jnp.float32).reshape(256, 128)
    odd = land[1].astype(jnp.float32).reshape(256, 128)
    half0 = jnp.where(low, even, pltpu.roll(odd, 32, 1)).reshape(4, 8, 8, 128)
    half1 = jnp.where(low, pltpu.roll(even, 96, 1), odd).reshape(4, 8, 8, 128)
    lane = lax.broadcasted_iota(jnp.int32, (CD, 128), 1)
    real = (lane // 16) % 2 == 0
    tiles = {}
    for i in range(4):
        for p in range(8):
            tile = jnp.concatenate([half0[i, p], half1[i, p]], axis=0)
            both[h, i, k, :, 128 * p : 128 * p + 128] = tile.astype(jnp.bfloat16)
            tiles[i, p] = tile

    pending = []

    def send(src, dst, to, send_sem, recv_sem):
        copy = pltpu.make_async_remote_copy(
            src_ref=src,
            dst_ref=dst,
            send_sem=send_sem,
            recv_sem=recv_sem,
            device_id=(t, to),
            device_id_type=MESH,
        )
        copy.start()
        pending.append(copy)

    def landed(ref, sem):
        pltpu.make_async_copy(ref, ref, sem).wait()

    def piece(dh, a, core):
        return both.at[(h + dh) % 4, pl.ds(2 * a, 2), core]

    def along_y(dh, a, by, send_sem):
        seen_as = (dh - by) % 4
        ref = piece(dh, a, k)
        send(ref, ref, chan(by, 0), send_sem, ry.at[seen_as - 1, a])

    def to_partner(dh, a):
        ref = piece(dh, a, k)
        send(ref, ref, partner, sp.at[dh, a], rp.at[dh, a])

    along_y(0, 0, 1, sy.at[0, 0])
    along_y(0, 1, 3, sy.at[1, 1])
    to_partner(0, 0)
    to_partner(0, 1)
    along_y(0, 1, 1, sy.at[0, 1])
    along_y(0, 0, 3, sy.at[1, 0])

    for (i, p), tile in tiles.items():
        flipped = jnp.where(real, pltpu.roll(tile, 112, 1), -pltpu.roll(tile, 16, 1))
        for r, source in enumerate((tile, flipped)):
            for b in range(2):
                kept = jnp.where(lane // 64 == b, source, 0.0).astype(jnp.bfloat16)
                left[r, b, i, :, 128 * p : 128 * p + 128] = kept

    def columns(dh):
        return pl.ds(pl.multiple_of(((h + dh) % 4) * 128, 128), 128)

    def compute(dh):
        for a in range(2):
            landed(piece(dh, a, 1 - k), rp.at[dh, a])
        part = lax.dot_general(
            left[...].reshape(256, 1024),
            both[(h + dh) % 4].reshape(128, 1024),
            (((1,), (1,)), ((), ())),
            preferred_element_type=jnp.float32,
        )
        result[dh] = part.reshape(2, 2, 4, CD, 128)
        bins = pl.ds(2 * x, 2)
        for e in (2, 1, 3):
            send(
                result.at[dh, :, :, (x + e) % 4],
                out.at[:, bins, :, columns(dh)],
                chan(0, e),
                so.at[dh, e],
                ro.at[dh, e],
            )
        stay = pltpu.make_async_copy(
            result.at[dh, :, :, x], out.at[:, bins, :, columns(dh)], so.at[dh, 0]
        )
        stay.start()
        return stay

    stays = [compute(0)]
    landed(piece(3, 0, k), ry.at[2, 0])
    along_y(3, 0, 1, sy.at[2, 0])
    to_partner(3, 0)
    landed(piece(1, 1, k), ry.at[0, 1])
    along_y(1, 1, 3, sy.at[2, 1])
    to_partner(1, 1)
    landed(piece(3, 1, k), ry.at[2, 1])
    to_partner(3, 1)
    landed(piece(1, 0, k), ry.at[0, 0])
    to_partner(1, 0)
    stays.append(compute(3))
    stays.append(compute(1))
    landed(piece(2, 0, k), ry.at[1, 0])
    to_partner(2, 0)
    landed(piece(2, 1, k), ry.at[1, 1])
    to_partner(2, 1)
    stays.append(compute(2))
    for dh in (0, 3, 1, 2):
        for e in (1, 2, 3):
            landed(out.at[:, pl.ds(2 * ((x - e) % 4), 2), :, columns(dh)], ro.at[dh, e])
    for copy in pending:
        copy.wait_send()
    for stay in stays:
        stay.wait()
    pltpu.make_async_copy(count, count, s1).wait()


def cross(packed):
    dma = pltpu.SemaphoreType.DMA
    bf16, f32 = jnp.bfloat16, jnp.float32
    return pl.pallas_call(
        cross_kernel,
        out_shape=jax.ShapeDtypeStruct((2, 8, CD, 512), f32),
        in_specs=[pl.BlockSpec(memory_space=pltpu.VMEM)],
        out_specs=pl.BlockSpec(memory_space=pl.ANY),
        scratch_shapes=[
            pltpu.VMEM((2, 4, 8, 8, 128), bf16),
            pltpu.VMEM((PAIRS, 8, 128), bf16),
            pltpu.VMEM((4, 4, 2, CD, 1024), bf16),
            pltpu.VMEM((2, 2, 4, CD, 1024), bf16),
            pltpu.VMEM((4, 2, 2, 4, CD, 128), f32),
            dma(()),
            dma(()),
            dma(()),
            dma((3, 2)),
            dma((3, 2)),
            dma((4, 2)),
            dma((4, 2)),
            dma((4, 4)),
            dma((4, 4)),
        ],
        compiler_params=pltpu.CompilerParams(
            vmem_limit_bytes=40 * 1024 * 1024, collective_id=0, has_side_effects=True
        ),
        name="cross",
    )(packed)


def on_device(raw):
    stored, packed = front(raw)
    totals = cross(packed.reshape(16, 4, 8, 128))
    return stored.reshape(F, CD, 2 * WD), totals * jnp.float32(1.0 / (16 * WD))


def solution(mesh):
    return jax.shard_map(
        on_device,
        mesh=mesh,
        in_specs=(P("chan", "tm"),),
        out_specs=(P(None, "chan", "tm"), P(None, "tm", "chan", None)),
        check_vma=False,
    )
```

```python
import math

import jax
import jax.numpy as jnp
import numpy as np
from jax import lax
from jax.experimental import pallas as pl
from jax.experimental.pallas import tpu as pltpu
from jax.sharding import PartitionSpec as P

L = 2000
F = 128
K0 = 8
RM = 250
SMOOTH = 16
HOP = 1000
CD = 16
WD = 16
LEAD = 256
TAIL = 1280
NBLK = 67
KP = 1024
PAIRS = 64
MESH = pl.DeviceIdType.MESH


def bin_order():
    return (np.arange(PAIRS)[None, :] * 2 + np.arange(2)[:, None]).reshape(-1)


def build_table():
    sample_ids = np.arange(L, dtype=np.int64)[:, None]
    bin_ids = (K0 + np.arange(F, dtype=np.int64))[None, :]
    turns = (sample_ids * bin_ids % L).astype(np.float32) * np.float32(2.0 * math.pi / L)
    both = np.stack([np.cos(turns), -np.sin(turns)], axis=0)
    both = both[:, :, bin_order()].transpose(0, 2, 1).reshape(2 * F, 2, HOP)
    out = np.zeros((2, 2 * F, KP), np.float32)
    out[:, :, :HOP] = both.transpose(1, 0, 2)
    return jnp.asarray(out.astype(jnp.bfloat16))


def build_kernel():
    positions = np.arange(F, dtype=np.float32)
    distance = positions[:, None] - positions[None, :]
    weights = np.exp(-distance * distance / np.float32(2.0 * SMOOTH * SMOOTH))
    weights = weights / np.sum(weights, axis=1, keepdims=True, dtype=np.float32)
    order = bin_order()
    return jnp.asarray(weights[order][:, order].astype(np.float32))


def build_band():
    i = np.arange(3 * 256)[:, None]
    j = np.arange(256)[None, :]
    first = LEAD - RM
    band = (i - j >= first) & (i - j <= first + 2 * RM)
    return jnp.asarray(band.astype(np.float32).astype(jnp.bfloat16))


def build_swap():
    out = np.zeros((256, 256), np.float32)
    for w in range(WD):
        for c in range(CD):
            out[w * CD + c, c * WD + w] = 1.0
    return jnp.asarray(out.astype(jnp.bfloat16))


def halo_kernel(raw, lead, tail, send_sem, recv_sem):
    t = lax.axis_index("tm")
    c = lax.axis_index("chan")
    after, before = (t + 1) % 16, (t + 15) % 16
    barrier = pltpu.get_barrier_semaphore()
    for other in (after, before):
        pl.semaphore_signal(barrier, inc=1, device_id=(other, c), device_id_type=MESH)
    pl.semaphore_wait(barrier, 2)
    halos = []
    for n, (first, count, dst, other) in enumerate(
        ((raw.shape[1] - LEAD, LEAD, lead, after), (0, TAIL, tail, before))
    ):
        halo = pltpu.make_async_remote_copy(
            src_ref=raw.at[:, first : first + count],
            dst_ref=dst,
            send_sem=send_sem.at[n],
            recv_sem=recv_sem.at[n],
            device_id=(other, c),
            device_id_type=MESH,
        )
        halo.start()
        halos.append(halo)
    for halo in halos:
        halo.wait()


def exchange_rims(raw):
    anywhere = pl.BlockSpec(memory_space=pl.ANY)
    dma = pltpu.SemaphoreType.DMA
    return pl.pallas_call(
        halo_kernel,
        out_shape=(
            jax.ShapeDtypeStruct((CD, LEAD), raw.dtype),
            jax.ShapeDtypeStruct((CD, TAIL), raw.dtype),
        ),
        in_specs=[anywhere],
        out_specs=(anywhere, anywhere),
        scratch_shapes=[dma((2,)), dma((2,))],
        compiler_params=pltpu.CompilerParams(collective_id=1, has_side_effects=True),
        name="rims",
    )(raw)


def front_part(
    t, hbm, raw, lead, tail, table, kern, band, swap, ext, norm, pieces, mid, packed, load_sem
):
    loads = []
    for n, (src, dst) in enumerate(zip(hbm, (raw, lead, tail, band, table, kern, swap))):
        load = pltpu.make_async_copy(src, dst, load_sem.at[n])
        load.start()
        loads.append(load)
    for load in loads[:3]:
        load.wait()
    for i in range(62):
        ext[1 + i] = raw[:, 256 * i : 256 * i + 256]
    ext[63, :, 0:128] = raw[:, 15872:16000]
    ext[68, :, 128:256] = jnp.zeros((CD, 128), jnp.bfloat16)
    has_lead = jnp.full((CD, LEAD), t, jnp.int32) > 0
    has_tail = jnp.full((CD, TAIL), t, jnp.int32) < 15
    ext[0] = jnp.where(has_lead, lead[...].astype(jnp.float32), 0.0).astype(jnp.bfloat16)
    behind = jnp.where(has_tail, tail[...].astype(jnp.float32), 0.0).astype(jnp.bfloat16)
    ext[63, :, 128:256] = behind[:, 0:128]
    for j in range(4):
        ext[64 + j] = behind[:, 128 + 256 * j : 384 + 256 * j]
    ext[68, :, 0:128] = behind[:, 1152:1280]
    for load in loads[3:]:
        load.wait()

    box = jnp.zeros((NBLK * CD, 256), jnp.float32)
    for d in range(3):
        box += jnp.dot(
            jnp.abs(ext[d : d + NBLK]).reshape(NBLK * CD, 256),
            band[256 * d : 256 * d + 256, :],
            preferred_element_type=jnp.float32,
        )
    inner = ext[1 : 1 + NBLK].reshape(NBLK * CD, 256).astype(jnp.float32)
    value = inner / (box * jnp.float32(1.0 / (2 * RM + 1)) + jnp.float32(1e-6))
    for i in range(NBLK):
        norm[:, 256 * i : 256 * i + 256] = value[CD * i : CD * i + CD, :]
    for p in range(WD + 1):
        start = p * HOP // 128 * 128
        off = p * HOP - start
        wide = norm[:, start : start + 1152]
        if off:
            wide = pltpu.roll(wide, 1152 - off, 1)
        pieces[CD * p : CD * p + CD, :] = wide[:, :KP].astype(jnp.bfloat16)

    contract = (((1,), (1,)), ((), ()))
    spec = lax.dot_general(
        table[0], pieces[0 : WD * CD, :], contract, preferred_element_type=jnp.float32
    ) + lax.dot_general(
        table[1], pieces[CD : CD + WD * CD, :], contract, preferred_element_type=jnp.float32
    )
    energy = spec[:F] * spec[:F] + spec[F:] * spec[F:]
    smoothed = jnp.dot(
        kern[...], energy, precision=lax.Precision.HIGHEST, preferred_element_type=jnp.float32
    )
    scale = lax.rsqrt(smoothed + jnp.float32(1e-6))
    white = (spec * jnp.concatenate([scale, scale], axis=0)).astype(jnp.bfloat16)
    turned = jnp.dot(white, swap[...], preferred_element_type=jnp.float32)
    group = lax.broadcasted_iota(jnp.int32, (PAIRS, 128), 1) // 16
    parts = []
    for b in range(2):
        for half in range(2):
            for r in range(2):
                row = r * F + b * PAIRS
                part = turned[row : row + PAIRS, half * 128 : half * 128 + 128]
                slot = len(parts)
                parts.append(pltpu.roll(part, 16 * slot, 1) if slot else part)
    for ih in range(8):
        line = parts[0]
        for slot in range(1, 8):
            line = jnp.where(group == (ih + slot) % 8, parts[slot], line)
        if ih:
            line = pltpu.roll(line, 128 - 16 * ih, 1)
        mid[pl.ds(ih, PAIRS, stride=8), :] = line
    everything = mid[...]
    packed[...] = everything.reshape(16, 4, 8, 128).astype(jnp.bfloat16)
    return white

def store_part(white, swap, stored):
    row = lax.broadcasted_iota(jnp.int32, (F, F), 0)
    column = lax.broadcasted_iota(jnp.int32, (F, F), 1)
    order = jnp.where(column == 2 * (row % PAIRS) + row // PAIRS, 1.0, 0.0).astype(jnp.bfloat16)
    for r in range(2):
        turned = lax.dot_general(
            swap[...],
            white[r * F : r * F + F],
            (((1,), (1,)), ((), ())),
            preferred_element_type=jnp.float32,
        ).astype(jnp.bfloat16)
        turned = jnp.dot(turned, order, preferred_element_type=jnp.float32)
        stored[:, r * WD : r * WD + WD, :] = turned.reshape(CD, WD, F).astype(jnp.bfloat16)


def main_kernel(
    raw_hbm, lead_hbm, tail_hbm, band_hbm, table_hbm, kern_hbm, swap_hbm, stored, out,
    raw, lead, tail, table, kern, band, swap, ext, norm, pieces, mid, packed,
    land, flat, both, left, result, load_sem, own_sem, s1, r1, sy, ry, sp, rp, so, ro
):
    t = lax.axis_index("tm")
    c = lax.axis_index("chan")
    h, x, k = c // 8, (c // 2) % 4, c % 2

    def chan(dh, dx):
        return ((h + dh) % 4) * 8 + ((x + dx) % 4) * 2 + k

    partner = c + 1 - 2 * k
    others = [(dt, dx) for dx in range(4) for dt in range(16) if dt or dx]
    barrier = pltpu.get_barrier_semaphore()
    for dt, dx in others:
        pl.semaphore_signal(
            barrier, inc=1, device_id=((t + dt) % 16, chan(0, dx)), device_id_type=MESH
        )
    for other in (chan(1, 0), chan(3, 0), partner):
        pl.semaphore_signal(barrier, inc=1, device_id=(t, other), device_id_type=MESH)
    hbm = (raw_hbm, lead_hbm, tail_hbm, band_hbm, table_hbm, kern_hbm, swap_hbm)
    white = front_part(
        t, hbm, raw, lead, tail, table, kern, band, swap, ext, norm, pieces, mid, packed, load_sem
    )
    pl.semaphore_wait(barrier, len(others) + 3)

    place = land.at[t % 2, x, t // 2]
    own = pltpu.make_async_copy(packed.at[t, x], place, own_sem)
    own.start()
    for dt, dx in others:
        to_t, to_x = (t + dt) % 16, (x + dx) % 4
        pltpu.make_async_remote_copy(
            src_ref=packed.at[to_t, to_x],
            dst_ref=place,
            send_sem=s1,
            recv_sem=r1,
            device_id=(to_t, chan(0, dx)),
            device_id_type=MESH,
        ).start()
    own.wait()
    store_part(white, swap, stored)
    count = flat.at[pl.ds(0, len(others))]
    pltpu.make_async_copy(count, count, r1).wait()

    lane = lax.broadcasted_iota(jnp.int32, (256, 128), 1)
    low = (lane // 32) % 2 == 0
    even = land[0].astype(jnp.float32).reshape(256, 128)
    odd = land[1].astype(jnp.float32).reshape(256, 128)
    half0 = jnp.where(low, even, pltpu.roll(odd, 32, 1)).reshape(4, 8, 8, 128)
    half1 = jnp.where(low, pltpu.roll(even, 96, 1), odd).reshape(4, 8, 8, 128)
    lane = lax.broadcasted_iota(jnp.int32, (CD, 128), 1)
    real = (lane // 16) % 2 == 0
    tiles = {}
    for i in range(4):
        for p in range(8):
            tile = jnp.concatenate([half0[i, p], half1[i, p]], axis=0)
            both[h, i, k, :, 128 * p : 128 * p + 128] = tile.astype(jnp.bfloat16)
            tiles[i, p] = tile

    pending = []

    def send(src, dst, to, send_sem, recv_sem):
        copy = pltpu.make_async_remote_copy(
            src_ref=src,
            dst_ref=dst,
            send_sem=send_sem,
            recv_sem=recv_sem,
            device_id=(t, to),
            device_id_type=MESH,
        )
        copy.start()
        pending.append(copy)

    def landed(ref, sem):
        pltpu.make_async_copy(ref, ref, sem).wait()

    def piece(dh, a, core):
        return both.at[(h + dh) % 4, pl.ds(1 * a, 1), core]

    def along_y(dh, a, by, send_sem):
        seen_as = (dh - by) % 4
        ref = piece(dh, a, k)
        send(ref, ref, chan(by, 0), send_sem, ry.at[seen_as - 1, a])

    def to_partner(dh, a):
        ref = piece(dh, a, k)
        send(ref, ref, partner, sp.at[dh, a], rp.at[dh, a])

    along_y(0, 0, 1, sy.at[0, 0])
    along_y(0, 2, 3, sy.at[1, 2])
    to_partner(0, 0)
    along_y(0, 1, 1, sy.at[0, 1])
    along_y(0, 3, 3, sy.at[1, 3])
    to_partner(0, 1)
    along_y(0, 2, 1, sy.at[0, 2])
    along_y(0, 0, 3, sy.at[1, 0])
    to_partner(0, 2)
    along_y(0, 3, 1, sy.at[0, 3])
    along_y(0, 1, 3, sy.at[1, 1])
    to_partner(0, 3)

    for (i, p), tile in tiles.items():
        flipped = jnp.where(real, pltpu.roll(tile, 112, 1), -pltpu.roll(tile, 16, 1))
        for r, source in enumerate((tile, flipped)):
            for b in range(2):
                kept = jnp.where(lane // 64 == b, source, 0.0).astype(jnp.bfloat16)
                left[r, b, i, :, 128 * p : 128 * p + 128] = kept

    def columns(dh):
        return pl.ds(pl.multiple_of(((h + dh) % 4) * 128, 128), 128)

    def compute(dh):
        for a in range(4):
            landed(piece(dh, a, 1 - k), rp.at[dh, a])
        part = lax.dot_general(
            left[...].reshape(256, 1024),
            both[(h + dh) % 4].reshape(128, 1024),
            (((1,), (1,)), ((), ())),
            preferred_element_type=jnp.float32,
        )
        result[dh] = part.reshape(2, 2, 4, CD, 128)
        bins = pl.ds(2 * x, 2)
        for e in (2, 1, 3):
            send(
                result.at[dh, :, :, (x + e) % 4],
                out.at[:, bins, :, columns(dh)],
                chan(0, e),
                so.at[dh, e],
                ro.at[dh, e],
            )
        stay = pltpu.make_async_copy(
            result.at[dh, :, :, x], out.at[:, bins, :, columns(dh)], so.at[dh, 0]
        )
        stay.start()
        return stay

    stays = [compute(0)]
    landed(piece(3, 0, k), ry.at[2, 0])
    along_y(3, 0, 1, sy.at[2, 0])
    to_partner(3, 0)
    landed(piece(1, 2, k), ry.at[0, 2])
    along_y(1, 2, 3, sy.at[2, 2])
    to_partner(1, 2)
    landed(piece(3, 1, k), ry.at[2, 1])
    along_y(3, 1, 1, sy.at[2, 1])
    to_partner(3, 1)
    landed(piece(1, 3, k), ry.at[0, 3])
    along_y(1, 3, 3, sy.at[2, 3])
    to_partner(1, 3)
    landed(piece(3, 2, k), ry.at[2, 2])
    to_partner(3, 2)
    landed(piece(1, 0, k), ry.at[0, 0])
    to_partner(1, 0)
    landed(piece(3, 3, k), ry.at[2, 3])
    to_partner(3, 3)
    landed(piece(1, 1, k), ry.at[0, 1])
    to_partner(1, 1)
    stays.append(compute(3))
    stays.append(compute(1))
    landed(piece(2, 0, k), ry.at[1, 0])
    to_partner(2, 0)
    landed(piece(2, 2, k), ry.at[1, 2])
    to_partner(2, 2)
    landed(piece(2, 1, k), ry.at[1, 1])
    to_partner(2, 1)
    landed(piece(2, 3, k), ry.at[1, 3])
    to_partner(2, 3)
    stays.append(compute(2))
    for dh in (0, 3, 1, 2):
        for e in (1, 2, 3):
            landed(out.at[:, pl.ds(2 * ((x - e) % 4), 2), :, columns(dh)], ro.at[dh, e])
    for copy in pending:
        copy.wait_send()
    for stay in stays:
        stay.wait()
    pltpu.make_async_copy(count, count, s1).wait()


def main(raw, lead, tail):
    vm = pl.BlockSpec(memory_space=pltpu.VMEM)
    anywhere = pl.BlockSpec(memory_space=pl.ANY)
    dma = pltpu.SemaphoreType.DMA
    bf16, f32 = jnp.bfloat16, jnp.float32
    return pl.pallas_call(
        main_kernel,
        out_shape=(
            jax.ShapeDtypeStruct((CD, 2 * WD, F), bf16),
            jax.ShapeDtypeStruct((2, 8, CD, 512), f32),
        ),
        in_specs=[anywhere] * 7,
        out_specs=(vm, anywhere),
        scratch_shapes=[
            pltpu.VMEM(raw.shape, bf16),
            pltpu.VMEM((CD, LEAD), bf16),
            pltpu.VMEM((CD, TAIL), bf16),
            pltpu.VMEM((2, 2 * F, KP), bf16),
            pltpu.VMEM((F, F), f32),
            pltpu.VMEM((768, 256), bf16),
            pltpu.VMEM((256, 256), bf16),
            pltpu.VMEM((NBLK + 2, CD, 256), bf16),
            pltpu.VMEM((CD, 17280), f32),
            pltpu.VMEM((CD * (WD + 1), KP), bf16),
            pltpu.VMEM((512, 128), f32),
            pltpu.VMEM((16, 4, 8, 128), bf16),
            pltpu.VMEM((2, 4, 8, 8, 128), bf16),
            pltpu.VMEM((PAIRS, 8, 128), bf16),
            pltpu.VMEM((4, 4, 2, CD, 1024), bf16),
            pltpu.VMEM((2, 2, 4, CD, 1024), bf16),
            pltpu.VMEM((4, 2, 2, 4, CD, 128), f32),
            dma((7,)),
            dma(()),
            dma(()),
            dma(()),
            dma((3, 4)),
            dma((3, 4)),
            dma((4, 4)),
            dma((4, 4)),
            dma((4, 4)),
            dma((4, 4)),
        ],
        compiler_params=pltpu.CompilerParams(
            vmem_limit_bytes=58 * 1024 * 1024, collective_id=0, has_side_effects=True
        ),
        name="main",
    )(raw, lead, tail, build_band(), build_table(), build_kernel(), build_swap())


def on_device(raw):
    stored, totals = main(raw, *exchange_rims(raw))
    return jnp.transpose(stored, (2, 0, 1)), totals * jnp.float32(1.0 / (16 * WD))


def solution(mesh):
    return jax.shard_map(
        on_device,
        mesh=mesh,
        in_specs=(P("chan", "tm"),),
        out_specs=(P(None, "chan", "tm"), P(None, "tm", "chan", None)),
        check_vma=False,
    )
```

```python
import math

import jax
import jax.numpy as jnp
import numpy as np
from jax import lax
from jax.experimental import pallas as pl
from jax.experimental.pallas import tpu as pltpu
from jax.sharding import PartitionSpec as P

L = 2000
F = 128
K0 = 8
RM = 250
SMOOTH = 16
HOP = 1000
CD = 16
WD = 16
LEAD = 256
TAIL = 1280
NBLK = 67
KP = 1024
PAIRS = 64
MESH = pl.DeviceIdType.MESH


def bin_order():
    return (np.arange(PAIRS)[None, :] * 2 + np.arange(2)[:, None]).reshape(-1)


def build_table():
    sample_ids = np.arange(L, dtype=np.int64)[:, None]
    bin_ids = (K0 + np.arange(F, dtype=np.int64))[None, :]
    turns = (sample_ids * bin_ids % L).astype(np.float32) * np.float32(2.0 * math.pi / L)
    both = np.stack([np.cos(turns), -np.sin(turns)], axis=0)
    both = both[:, :, bin_order()].transpose(0, 2, 1).reshape(2 * F, 2, HOP)
    out = np.zeros((2, 2 * F, KP), np.float32)
    out[:, :, :HOP] = both.transpose(1, 0, 2)
    return jnp.asarray(out.astype(jnp.bfloat16))


def halo_kernel(raw, rims, send_sem, recv_sem):
    t = lax.axis_index("tm")
    c = lax.axis_index("chan")
    after, before = (t + 1) % 16, (t + 15) % 16
    barrier = pltpu.get_barrier_semaphore()
    for other in (after, before):
        pl.semaphore_signal(barrier, inc=1, device_id=(other, c), device_id_type=MESH)
    pl.semaphore_wait(barrier, 2)
    halos = []
    for n, (first, count, dst, other) in enumerate(
        ((raw.shape[1] - LEAD, LEAD, 0, after), (0, TAIL, LEAD, before))
    ):
        halo = pltpu.make_async_remote_copy(
            src_ref=raw.at[:, first : first + count],
            dst_ref=rims.at[:, dst : dst + count],
            send_sem=send_sem.at[n],
            recv_sem=recv_sem.at[n],
            device_id=(other, c),
            device_id_type=MESH,
        )
        halo.start()
        halos.append(halo)
    for halo in halos:
        halo.wait()


def exchange_rims(raw):
    anywhere = pl.BlockSpec(memory_space=pl.ANY)
    dma = pltpu.SemaphoreType.DMA
    return pl.pallas_call(
        halo_kernel,
        out_shape=jax.ShapeDtypeStruct((CD, LEAD + TAIL), raw.dtype),
        in_specs=[anywhere],
        out_specs=anywhere,
        scratch_shapes=[dma((2,)), dma((2,))],
        compiler_params=pltpu.CompilerParams(
            vmem_limit_bytes=54784 * 1024, collective_id=1, has_side_effects=True
        ),
        name="rims",
    )(raw)


def front_part(
    t, hbm, raw, rims, table, kern, band, swap, ext, norm, pieces, mid, packed, load_sem
):
    loads = []
    for n, (src, dst) in enumerate(zip(hbm, (raw, rims, table))):
        load = pltpu.make_async_copy(src, dst, load_sem.at[n])
        load.start()
        loads.append(load)
    row = lax.broadcasted_iota(jnp.int32, (F, F), 0)
    column = lax.broadcasted_iota(jnp.int32, (F, F), 1)
    apart = 2 * (row % PAIRS) + row // PAIRS - 2 * (column % PAIRS) - column // PAIRS
    apart = apart.astype(jnp.float32)
    weights = jnp.exp(-apart * apart / jnp.float32(2.0 * SMOOTH * SMOOTH))
    kern[...] = weights / jnp.sum(weights, axis=1, keepdims=True)
    row = lax.broadcasted_iota(jnp.int32, (256, 256), 0)
    column = lax.broadcasted_iota(jnp.int32, (256, 256), 1)
    turn = column == row % CD * WD + row // CD
    swap[...] = jnp.where(turn, 1.0, 0.0).astype(jnp.bfloat16)
    row = lax.broadcasted_iota(jnp.int32, (3 * 256, 256), 0)
    column = lax.broadcasted_iota(jnp.int32, (3 * 256, 256), 1)
    inside = jnp.abs(row - column - LEAD) <= RM
    band[...] = jnp.where(inside, 1.0, 0.0).astype(jnp.bfloat16)
    for load in loads[:2]:
        load.wait()
    for i in range(62):
        ext[1 + i] = raw[:, 256 * i : 256 * i + 256]
    ext[63, :, 0:128] = raw[:, 15872:16000]
    ext[68, :, 128:256] = jnp.zeros((CD, 128), jnp.bfloat16)
    has_lead = jnp.full((CD, LEAD), t, jnp.int32) > 0
    has_tail = jnp.full((CD, TAIL), t, jnp.int32) < 15
    ext[0] = jnp.where(has_lead, rims[:, :LEAD].astype(jnp.float32), 0.0).astype(jnp.bfloat16)
    behind = jnp.where(has_tail, rims[:, LEAD:].astype(jnp.float32), 0.0).astype(jnp.bfloat16)
    ext[63, :, 128:256] = behind[:, 0:128]
    for j in range(4):
        ext[64 + j] = behind[:, 128 + 256 * j : 384 + 256 * j]
    ext[68, :, 0:128] = behind[:, 1152:1280]
    for load in loads[2:]:
        load.wait()

    box = jnp.zeros((NBLK * CD, 256), jnp.float32)
    for d in range(3):
        box += jnp.dot(
            jnp.abs(ext[d : d + NBLK]).reshape(NBLK * CD, 256),
            band[256 * d : 256 * d + 256, :],
            preferred_element_type=jnp.float32,
        )
    inner = ext[1 : 1 + NBLK].reshape(NBLK * CD, 256).astype(jnp.float32)
    value = inner / (box * jnp.float32(1.0 / (2 * RM + 1)) + jnp.float32(1e-6))
    for i in range(NBLK):
        norm[:, 256 * i : 256 * i + 256] = value[CD * i : CD * i + CD, :]
    for p in range(WD + 1):
        start = p * HOP // 128 * 128
        off = p * HOP - start
        wide = norm[:, start : start + 1152]
        if off:
            wide = pltpu.roll(wide, 1152 - off, 1)
        pieces[CD * p : CD * p + CD, :] = wide[:, :KP].astype(jnp.bfloat16)

    contract = (((1,), (1,)), ((), ()))
    spec = lax.dot_general(
        table[0], pieces[0 : WD * CD, :], contract, preferred_element_type=jnp.float32
    ) + lax.dot_general(
        table[1], pieces[CD : CD + WD * CD, :], contract, preferred_element_type=jnp.float32
    )
    energy = spec[:F] * spec[:F] + spec[F:] * spec[F:]
    smoothed = jnp.dot(
        kern[...], energy, precision=lax.Precision.HIGHEST, preferred_element_type=jnp.float32
    )
    scale = lax.rsqrt(smoothed + jnp.float32(1e-6))
    white = (spec * jnp.concatenate([scale, scale], axis=0)).astype(jnp.bfloat16)
    turned = jnp.dot(white, swap[...], preferred_element_type=jnp.float32)
    group = lax.broadcasted_iota(jnp.int32, (PAIRS, 128), 1) // 16
    parts = []
    for b in range(2):
        for half in range(2):
            for r in range(2):
                row = r * F + b * PAIRS
                part = turned[row : row + PAIRS, half * 128 : half * 128 + 128]
                slot = len(parts)
                parts.append(pltpu.roll(part, 16 * slot, 1) if slot else part)
    for ih in range(8):
        line = parts[0]
        for slot in range(1, 8):
            line = jnp.where(group == (ih + slot) % 8, parts[slot], line)
        if ih:
            line = pltpu.roll(line, 128 - 16 * ih, 1)
        mid[pl.ds(ih, PAIRS, stride=8), :] = line
    everything = mid[...]
    packed[...] = everything.reshape(16, 4, 8, 128).astype(jnp.bfloat16)
    return white

def store_part(white, swap, stored):
    row = lax.broadcasted_iota(jnp.int32, (F, F), 0)
    column = lax.broadcasted_iota(jnp.int32, (F, F), 1)
    order = jnp.where(column == 2 * (row % PAIRS) + row // PAIRS, 1.0, 0.0).astype(jnp.bfloat16)
    for r in range(2):
        turned = lax.dot_general(
            swap[...],
            white[r * F : r * F + F],
            (((1,), (1,)), ((), ())),
            preferred_element_type=jnp.float32,
        ).astype(jnp.bfloat16)
        turned = jnp.dot(turned, order, preferred_element_type=jnp.float32)
        stored[:, r * WD : r * WD + WD, :] = turned.reshape(CD, WD, F).astype(jnp.bfloat16)


def main_kernel(
    raw_hbm, rims_hbm, table_hbm, stored, out,
    raw, rims, table, kern, band, swap, ext, norm, pieces, mid, packed,
    land, flat, both, left, result, load_sem, own_sem, s1, r1, sy, ry, sp, rp, so, ro
):
    t = lax.axis_index("tm")
    c = lax.axis_index("chan")
    h, x, k = c // 8, (c // 2) % 4, c % 2

    def chan(dh, dx):
        return ((h + dh) % 4) * 8 + ((x + dx) % 4) * 2 + k

    partner = c + 1 - 2 * k
    others = [(dt, dx) for dx in range(4) for dt in range(16) if dt or dx]
    others.sort(key=lambda o: -min(o[0] % 8, 8 - o[0] % 8) - min(o[1], 4 - o[1]))
    barrier = pltpu.get_barrier_semaphore()
    for dt, dx in others:
        pl.semaphore_signal(
            barrier, inc=1, device_id=((t + dt) % 16, chan(0, dx)), device_id_type=MESH
        )
    for other in (chan(1, 0), chan(3, 0), partner):
        pl.semaphore_signal(barrier, inc=1, device_id=(t, other), device_id_type=MESH)
    hbm = (raw_hbm, rims_hbm, table_hbm)
    white = front_part(
        t, hbm, raw, rims, table, kern, band, swap, ext, norm, pieces, mid, packed, load_sem
    )
    pl.semaphore_wait(barrier, len(others) + 3)

    place = land.at[t % 2, x, t // 2]
    own = pltpu.make_async_copy(packed.at[t, x], place, own_sem)
    own.start()
    for dt, dx in others:
        to_t, to_x = (t + dt) % 16, (x + dx) % 4
        pltpu.make_async_remote_copy(
            src_ref=packed.at[to_t, to_x],
            dst_ref=place,
            send_sem=s1,
            recv_sem=r1,
            device_id=(to_t, chan(0, dx)),
            device_id_type=MESH,
        ).start()
    own.wait()
    store_part(white, swap, stored)
    count = flat.at[pl.ds(0, len(others))]
    pltpu.make_async_copy(count, count, r1).wait()

    lane = lax.broadcasted_iota(jnp.int32, (256, 128), 1)
    low = (lane // 32) % 2 == 0
    even = land[0].astype(jnp.float32).reshape(256, 128)
    odd = land[1].astype(jnp.float32).reshape(256, 128)
    half0 = jnp.where(low, even, pltpu.roll(odd, 32, 1)).reshape(4, 8, 8, 128)
    half1 = jnp.where(low, pltpu.roll(even, 96, 1), odd).reshape(4, 8, 8, 128)
    lane = lax.broadcasted_iota(jnp.int32, (CD, 128), 1)
    real = (lane // 16) % 2 == 0
    tiles = {}
    for i in range(4):
        for p in range(8):
            tile = jnp.concatenate([half0[i, p], half1[i, p]], axis=0)
            both[h, i, k, :, 128 * p : 128 * p + 128] = tile.astype(jnp.bfloat16)
            tiles[i, p] = tile

    pending = []

    def send(src, dst, to, send_sem, recv_sem):
        copy = pltpu.make_async_remote_copy(
            src_ref=src,
            dst_ref=dst,
            send_sem=send_sem,
            recv_sem=recv_sem,
            device_id=(t, to),
            device_id_type=MESH,
        )
        copy.start()
        pending.append(copy)

    def landed(ref, sem):
        pltpu.make_async_copy(ref, ref, sem).wait()

    def piece(dh, a, core):
        return both.at[(h + dh) % 4, pl.ds(1 * a, 1), core]

    def along_y(dh, a, by, send_sem):
        seen_as = (dh - by) % 4
        ref = piece(dh, a, k)
        send(ref, ref, chan(by, 0), send_sem, ry.at[seen_as - 1, a])

    def to_partner(dh, a):
        ref = piece(dh, a, k)
        send(ref, ref, partner, sp.at[dh, a], rp.at[dh, a])

    along_y(0, 0, 1, sy.at[0, 0])
    along_y(0, 2, 3, sy.at[1, 2])
    to_partner(0, 0)
    along_y(0, 1, 1, sy.at[0, 1])
    along_y(0, 3, 3, sy.at[1, 3])
    to_partner(0, 1)
    along_y(0, 2, 1, sy.at[0, 2])
    along_y(0, 0, 3, sy.at[1, 0])
    to_partner(0, 2)
    along_y(0, 3, 1, sy.at[0, 3])
    along_y(0, 1, 3, sy.at[1, 1])
    to_partner(0, 3)

    for (i, p), tile in tiles.items():
        flipped = jnp.where(real, pltpu.roll(tile, 112, 1), -pltpu.roll(tile, 16, 1))
        for r, source in enumerate((tile, flipped)):
            for b in range(2):
                kept = jnp.where(lane // 64 == b, source, 0.0).astype(jnp.bfloat16)
                left[r, b, i, :, 128 * p : 128 * p + 128] = kept

    def columns(dh):
        return pl.ds(pl.multiple_of(((h + dh) % 4) * 128, 128), 128)

    def compute(dh):
        for a in range(4):
            landed(piece(dh, a, 1 - k), rp.at[dh, a])
        part = lax.dot_general(
            left[...].reshape(256, 1024),
            both[(h + dh) % 4].reshape(128, 1024),
            (((1,), (1,)), ((), ())),
            preferred_element_type=jnp.float32,
        )
        result[dh] = part.reshape(2, 2, 4, CD, 128)
        bins = pl.ds(2 * x, 2)
        for e in (2, 1, 3):
            send(
                result.at[dh, :, :, (x + e) % 4],
                out.at[:, bins, :, columns(dh)],
                chan(0, e),
                so.at[dh, e],
                ro.at[dh, e],
            )
        stay = pltpu.make_async_copy(
            result.at[dh, :, :, x], out.at[:, bins, :, columns(dh)], so.at[dh, 0]
        )
        stay.start()
        return stay

    stays = []
    landed(piece(3, 0, k), ry.at[2, 0])
    along_y(3, 0, 1, sy.at[2, 0])
    to_partner(3, 0)
    landed(piece(1, 2, k), ry.at[0, 2])
    along_y(1, 2, 3, sy.at[2, 2])
    to_partner(1, 2)
    stays.append(compute(0))
    landed(piece(3, 1, k), ry.at[2, 1])
    along_y(3, 1, 1, sy.at[2, 1])
    to_partner(3, 1)
    landed(piece(1, 3, k), ry.at[0, 3])
    along_y(1, 3, 3, sy.at[2, 3])
    to_partner(1, 3)
    landed(piece(3, 2, k), ry.at[2, 2])
    to_partner(3, 2)
    landed(piece(1, 0, k), ry.at[0, 0])
    to_partner(1, 0)
    landed(piece(3, 3, k), ry.at[2, 3])
    to_partner(3, 3)
    landed(piece(1, 1, k), ry.at[0, 1])
    to_partner(1, 1)
    stays.append(compute(3))
    stays.append(compute(1))
    landed(piece(2, 0, k), ry.at[1, 0])
    to_partner(2, 0)
    landed(piece(2, 2, k), ry.at[1, 2])
    to_partner(2, 2)
    landed(piece(2, 1, k), ry.at[1, 1])
    to_partner(2, 1)
    landed(piece(2, 3, k), ry.at[1, 3])
    to_partner(2, 3)
    stays.append(compute(2))
    for dh in (0, 3, 1, 2):
        for e in (1, 2, 3):
            landed(out.at[:, pl.ds(2 * ((x - e) % 4), 2), :, columns(dh)], ro.at[dh, e])
    for copy in pending:
        copy.wait_send()
    for stay in stays:
        stay.wait()
    pltpu.make_async_copy(count, count, s1).wait()


def main(raw, rims):
    vm = pl.BlockSpec(memory_space=pltpu.VMEM)
    anywhere = pl.BlockSpec(memory_space=pl.ANY)
    dma = pltpu.SemaphoreType.DMA
    bf16, f32 = jnp.bfloat16, jnp.float32
    return pl.pallas_call(
        main_kernel,
        out_shape=(
            jax.ShapeDtypeStruct((CD, 2 * WD, F), bf16),
            jax.ShapeDtypeStruct((2, 8, CD, 512), f32),
        ),
        in_specs=[anywhere] * 3,
        out_specs=(vm, anywhere),
        scratch_shapes=[
            pltpu.VMEM(raw.shape, bf16),
            pltpu.VMEM(rims.shape, bf16),
            pltpu.VMEM((2, 2 * F, KP), bf16),
            pltpu.VMEM((F, F), f32),
            pltpu.VMEM((768, 256), bf16),
            pltpu.VMEM((256, 256), bf16),
            pltpu.VMEM((NBLK + 2, CD, 256), bf16),
            pltpu.VMEM((CD, 17280), f32),
            pltpu.VMEM((CD * (WD + 1), KP), bf16),
            pltpu.VMEM((512, 128), f32),
            pltpu.VMEM((16, 4, 8, 128), bf16),
            pltpu.VMEM((2, 4, 8, 8, 128), bf16),
            pltpu.VMEM((PAIRS, 8, 128), bf16),
            pltpu.VMEM((4, 4, 2, CD, 1024), bf16),
            pltpu.VMEM((2, 2, 4, CD, 1024), bf16),
            pltpu.VMEM((4, 2, 2, 4, CD, 128), f32),
            dma((3,)),
            dma(()),
            dma(()),
            dma(()),
            dma((3, 4)),
            dma((3, 4)),
            dma((4, 4)),
            dma((4, 4)),
            dma((4, 4)),
            dma((4, 4)),
        ],
        compiler_params=pltpu.CompilerParams(
            vmem_limit_bytes=53504 * 1024, collective_id=0, has_side_effects=True
        ),
        name="main",
    )(raw, rims, build_table())


def on_device(raw):
    stored, totals = main(raw, exchange_rims(raw))
    return jnp.transpose(stored, (2, 0, 1)), totals * jnp.float32(1.0 / (16 * WD))


def solution(mesh):
    return jax.shard_map(
        on_device,
        mesh=mesh,
        in_specs=(P("chan", "tm"),),
        out_specs=(P(None, "chan", "tm"), P(None, "tm", "chan", None)),
        check_vma=False,
    )
```

```python
import math

import jax
import jax.numpy as jnp
import numpy as np
from jax import lax
from jax.experimental import pallas as pl
from jax.experimental.pallas import tpu as pltpu
from jax.sharding import PartitionSpec as P

L = 2000
F = 128
K0 = 8
RM = 250
SMOOTH = 16
HOP = 1000
CD = 16
WD = 16
LEAD = 256
TAIL = 1280
NBLK = 67
KP = 1024
PAIRS = 64
MESH = pl.DeviceIdType.MESH


def bin_order():
    return (np.arange(PAIRS)[None, :] * 2 + np.arange(2)[:, None]).reshape(-1)


def build_table():
    sample_ids = np.arange(L, dtype=np.int64)[:, None]
    bin_ids = (K0 + np.arange(F, dtype=np.int64))[None, :]
    turns = (sample_ids * bin_ids % L).astype(np.float32) * np.float32(2.0 * math.pi / L)
    both = np.stack([np.cos(turns), -np.sin(turns)], axis=0)
    both = both[:, :, bin_order()].transpose(0, 2, 1).reshape(2 * F, 2, HOP)
    out = np.zeros((2, 2 * F, KP), np.float32)
    out[:, :, :HOP] = both.transpose(1, 0, 2)
    return jnp.asarray(out.astype(jnp.bfloat16))


def halo_kernel(raw, rims, send_sem, recv_sem):
    t = lax.axis_index("tm")
    c = lax.axis_index("chan")
    after, before = (t + 1) % 16, (t + 15) % 16
    barrier = pltpu.get_barrier_semaphore()
    for other in (after, before):
        pl.semaphore_signal(barrier, inc=1, device_id=(other, c), device_id_type=MESH)
    pl.semaphore_wait(barrier, 2)
    halos = []
    for n, (first, count, dst, other) in enumerate(
        ((raw.shape[1] - LEAD, LEAD, 0, after), (0, TAIL, LEAD, before))
    ):
        halo = pltpu.make_async_remote_copy(
            src_ref=raw.at[:, first : first + count],
            dst_ref=rims.at[:, dst : dst + count],
            send_sem=send_sem.at[n],
            recv_sem=recv_sem.at[n],
            device_id=(other, c),
            device_id_type=MESH,
        )
        halo.start()
        halos.append(halo)
    for halo in halos:
        halo.wait()


def exchange_rims(raw):
    anywhere = pl.BlockSpec(memory_space=pl.ANY)
    dma = pltpu.SemaphoreType.DMA
    return pl.pallas_call(
        halo_kernel,
        out_shape=jax.ShapeDtypeStruct((CD, LEAD + TAIL), raw.dtype),
        in_specs=[anywhere],
        out_specs=anywhere,
        scratch_shapes=[dma((2,)), dma((2,))],
        compiler_params=pltpu.CompilerParams(
            vmem_limit_bytes=54784 * 1024, collective_id=1, has_side_effects=True
        ),
        name="rims",
    )(raw)


def front_part(
    t, hbm, raw, rims, table, kern, band, swap, ext, norm, pieces, mid, packed, load_sem
):
    loads = []
    for n, (src, dst) in enumerate(zip(hbm, (raw, rims, table))):
        load = pltpu.make_async_copy(src, dst, load_sem.at[n])
        load.start()
        loads.append(load)
    row = lax.broadcasted_iota(jnp.int32, (F, F), 0)
    column = lax.broadcasted_iota(jnp.int32, (F, F), 1)
    apart = 2 * (row % PAIRS) + row // PAIRS - 2 * (column % PAIRS) - column // PAIRS
    apart = apart.astype(jnp.float32)
    weights = jnp.exp(-apart * apart / jnp.float32(2.0 * SMOOTH * SMOOTH))
    kern[...] = weights / jnp.sum(weights, axis=1, keepdims=True)
    row = lax.broadcasted_iota(jnp.int32, (256, 256), 0)
    column = lax.broadcasted_iota(jnp.int32, (256, 256), 1)
    turn = column == row % CD * WD + row // CD
    swap[...] = jnp.where(turn, 1.0, 0.0).astype(jnp.bfloat16)
    row = lax.broadcasted_iota(jnp.int32, (3 * 256, 256), 0)
    column = lax.broadcasted_iota(jnp.int32, (3 * 256, 256), 1)
    inside = jnp.abs(row - column - LEAD) <= RM
    band[...] = jnp.where(inside, 1.0, 0.0).astype(jnp.bfloat16)
    for load in loads[:2]:
        load.wait()
    for i in range(62):
        ext[1 + i] = raw[:, 256 * i : 256 * i + 256]
    ext[63, :, 0:128] = raw[:, 15872:16000]
    ext[68, :, 128:256] = jnp.zeros((CD, 128), jnp.bfloat16)
    has_lead = jnp.full((CD, LEAD), t, jnp.int32) > 0
    has_tail = jnp.full((CD, TAIL), t, jnp.int32) < 15
    ext[0] = jnp.where(has_lead, rims[:, :LEAD].astype(jnp.float32), 0.0).astype(jnp.bfloat16)
    behind = jnp.where(has_tail, rims[:, LEAD:].astype(jnp.float32), 0.0).astype(jnp.bfloat16)
    ext[63, :, 128:256] = behind[:, 0:128]
    for j in range(4):
        ext[64 + j] = behind[:, 128 + 256 * j : 384 + 256 * j]
    ext[68, :, 0:128] = behind[:, 1152:1280]
    box = jnp.zeros((NBLK * CD, 256), jnp.float32)
    for d in range(3):
        box += jnp.dot(
            jnp.abs(ext[d : d + NBLK]).reshape(NBLK * CD, 256),
            band[256 * d : 256 * d + 256, :],
            preferred_element_type=jnp.float32,
        )
    inner = ext[1 : 1 + NBLK].reshape(NBLK * CD, 256).astype(jnp.float32)
    value = inner / (box * jnp.float32(1.0 / (2 * RM + 1)) + jnp.float32(1e-6))
    for i in range(NBLK):
        norm[:, 256 * i : 256 * i + 256] = value[CD * i : CD * i + CD, :]
    for p in range(WD + 1):
        start = p * HOP // 128 * 128
        off = p * HOP - start
        wide = norm[:, start : start + 1152]
        if off:
            wide = pltpu.roll(wide, 1152 - off, 1)
        pieces[CD * p : CD * p + CD, :] = wide[:, :KP].astype(jnp.bfloat16)

    for load in loads[2:]:
        load.wait()
    contract = (((1,), (1,)), ((), ()))
    spec = lax.dot_general(
        table[0], pieces[0 : WD * CD, :], contract, preferred_element_type=jnp.float32
    ) + lax.dot_general(
        table[1], pieces[CD : CD + WD * CD, :], contract, preferred_element_type=jnp.float32
    )
    energy = spec[:F] * spec[:F] + spec[F:] * spec[F:]
    smoothed = jnp.dot(
        kern[...], energy, precision=lax.Precision.HIGHEST, preferred_element_type=jnp.float32
    )
    scale = lax.rsqrt(smoothed + jnp.float32(1e-6))
    white = (spec * jnp.concatenate([scale, scale], axis=0)).astype(jnp.bfloat16)
    turned = jnp.dot(white, swap[...], preferred_element_type=jnp.float32)
    group = lax.broadcasted_iota(jnp.int32, (PAIRS, 128), 1) // 16
    parts = []
    for b in range(2):
        for half in range(2):
            for r in range(2):
                row = r * F + b * PAIRS
                part = turned[row : row + PAIRS, half * 128 : half * 128 + 128]
                slot = len(parts)
                parts.append(pltpu.roll(part, 16 * slot, 1) if slot else part)
    for ih in range(8):
        line = parts[0]
        for slot in range(1, 8):
            line = jnp.where(group == (ih + slot) % 8, parts[slot], line)
        if ih:
            line = pltpu.roll(line, 128 - 16 * ih, 1)
        mid[pl.ds(ih, PAIRS, stride=8), :] = line
    everything = mid[...]
    packed[...] = everything.reshape(16, 4, 8, 128).astype(jnp.bfloat16)
    return white

def store_part(white, swap, stored):
    row = lax.broadcasted_iota(jnp.int32, (F, F), 0)
    column = lax.broadcasted_iota(jnp.int32, (F, F), 1)
    order = jnp.where(column == 2 * (row % PAIRS) + row // PAIRS, 1.0, 0.0).astype(jnp.bfloat16)
    for r in range(2):
        turned = lax.dot_general(
            swap[...],
            white[r * F : r * F + F],
            (((1,), (1,)), ((), ())),
            preferred_element_type=jnp.float32,
        ).astype(jnp.bfloat16)
        turned = jnp.dot(turned, order, preferred_element_type=jnp.float32)
        stored[:, r * WD : r * WD + WD, :] = turned.reshape(CD, WD, F).astype(jnp.bfloat16)


def main_kernel(
    raw_hbm, rims_hbm, table_hbm, stored, out,
    raw, rims, table, kern, band, swap, ext, norm, pieces, mid, packed,
    land, flat, both, left, result, load_sem, own_sem, s1, r1, sy, ry, sp, rp, so, ro
):
    t = lax.axis_index("tm")
    c = lax.axis_index("chan")
    h, x, k = c // 8, (c // 2) % 4, c % 2

    def chan(dh, dx):
        return ((h + dh) % 4) * 8 + ((x + dx) % 4) * 2 + k

    partner = c + 1 - 2 * k
    others = [(dt, dx) for dx in range(4) for dt in range(16) if dt or dx]
    others.sort(key=lambda o: -min(o[0] % 8, 8 - o[0] % 8) - min(o[1], 4 - o[1]))
    barrier = pltpu.get_barrier_semaphore()
    for dt, dx in others:
        pl.semaphore_signal(
            barrier, inc=1, device_id=((t + dt) % 16, chan(0, dx)), device_id_type=MESH
        )
    for other in (chan(1, 0), chan(3, 0), partner):
        pl.semaphore_signal(barrier, inc=1, device_id=(t, other), device_id_type=MESH)
    hbm = (raw_hbm, rims_hbm, table_hbm)
    white = front_part(
        t, hbm, raw, rims, table, kern, band, swap, ext, norm, pieces, mid, packed, load_sem
    )
    pl.semaphore_wait(barrier, len(others) + 3)

    place = land.at[t % 2, x, t // 2]
    own = pltpu.make_async_copy(packed.at[t, x], place, own_sem)
    own.start()
    for dt, dx in others:
        to_t, to_x = (t + dt) % 16, (x + dx) % 4
        pltpu.make_async_remote_copy(
            src_ref=packed.at[to_t, to_x],
            dst_ref=place,
            send_sem=s1,
            recv_sem=r1,
            device_id=(to_t, chan(0, dx)),
            device_id_type=MESH,
        ).start()
    own.wait()
    store_part(white, swap, stored)
    count = flat.at[pl.ds(0, len(others))]
    pltpu.make_async_copy(count, count, r1).wait()

    lane = lax.broadcasted_iota(jnp.int32, (256, 128), 1)
    low = (lane // 32) % 2 == 0
    even = land[0].astype(jnp.float32).reshape(256, 128)
    odd = land[1].astype(jnp.float32).reshape(256, 128)
    half0 = jnp.where(low, even, pltpu.roll(odd, 32, 1)).reshape(4, 8, 8, 128)
    half1 = jnp.where(low, pltpu.roll(even, 96, 1), odd).reshape(4, 8, 8, 128)
    lane = lax.broadcasted_iota(jnp.int32, (CD, 128), 1)
    real = (lane // 16) % 2 == 0
    tiles = {}
    for i in range(4):
        for p in range(8):
            tile = jnp.concatenate([half0[i, p], half1[i, p]], axis=0)
            both[h, i, k, :, 128 * p : 128 * p + 128] = tile.astype(jnp.bfloat16)
            tiles[i, p] = tile

    pending = []

    def send(src, dst, to, send_sem, recv_sem):
        copy = pltpu.make_async_remote_copy(
            src_ref=src,
            dst_ref=dst,
            send_sem=send_sem,
            recv_sem=recv_sem,
            device_id=(t, to),
            device_id_type=MESH,
        )
        copy.start()
        pending.append(copy)

    def landed(ref, sem):
        pltpu.make_async_copy(ref, ref, sem).wait()

    def piece(dh, a, core):
        return both.at[(h + dh) % 4, pl.ds(1 * a, 1), core]

    def along_y(dh, a, by, send_sem):
        seen_as = (dh - by) % 4
        ref = piece(dh, a, k)
        send(ref, ref, chan(by, 0), send_sem, ry.at[seen_as - 1, a])

    def to_partner(dh, a):
        ref = piece(dh, a, k)
        send(ref, ref, partner, sp.at[dh, a], rp.at[dh, a])

    along_y(0, 0, 1, sy.at[0, 0])
    along_y(0, 2, 3, sy.at[1, 2])
    to_partner(0, 0)
    along_y(0, 1, 1, sy.at[0, 1])
    along_y(0, 3, 3, sy.at[1, 3])
    to_partner(0, 1)
    along_y(0, 2, 1, sy.at[0, 2])
    along_y(0, 0, 3, sy.at[1, 0])
    to_partner(0, 2)
    along_y(0, 3, 1, sy.at[0, 3])
    along_y(0, 1, 3, sy.at[1, 1])
    to_partner(0, 3)

    for (i, p), tile in tiles.items():
        flipped = jnp.where(real, pltpu.roll(tile, 112, 1), -pltpu.roll(tile, 16, 1))
        for r, source in enumerate((tile, flipped)):
            for b in range(2):
                kept = jnp.where(lane // 64 == b, source, 0.0).astype(jnp.bfloat16)
                left[r, b, i, :, 128 * p : 128 * p + 128] = kept

    def columns(dh):
        return pl.ds(pl.multiple_of(((h + dh) % 4) * 128, 128), 128)

    def compute(dh):
        for a in range(4):
            landed(piece(dh, a, 1 - k), rp.at[dh, a])
        part = lax.dot_general(
            left[...].reshape(256, 1024),
            both[(h + dh) % 4].reshape(128, 1024),
            (((1,), (1,)), ((), ())),
            preferred_element_type=jnp.float32,
        )
        result[dh] = part.reshape(2, 2, 4, CD, 128)
        bins = pl.ds(2 * x, 2)
        for e in (2, 1, 3):
            send(
                result.at[dh, :, :, (x + e) % 4],
                out.at[:, bins, :, columns(dh)],
                chan(0, e),
                so.at[dh, e],
                ro.at[dh, e],
            )
        stay = pltpu.make_async_copy(
            result.at[dh, :, :, x], out.at[:, bins, :, columns(dh)], so.at[dh, 0]
        )
        stay.start()
        return stay

    stays = []
    landed(piece(3, 0, k), ry.at[2, 0])
    along_y(3, 0, 1, sy.at[2, 0])
    to_partner(3, 0)
    landed(piece(1, 2, k), ry.at[0, 2])
    along_y(1, 2, 3, sy.at[2, 2])
    to_partner(1, 2)
    stays.append(compute(0))
    landed(piece(3, 1, k), ry.at[2, 1])
    along_y(3, 1, 1, sy.at[2, 1])
    to_partner(3, 1)
    landed(piece(1, 3, k), ry.at[0, 3])
    along_y(1, 3, 3, sy.at[2, 3])
    to_partner(1, 3)
    landed(piece(3, 2, k), ry.at[2, 2])
    to_partner(3, 2)
    landed(piece(1, 0, k), ry.at[0, 0])
    to_partner(1, 0)
    landed(piece(3, 3, k), ry.at[2, 3])
    to_partner(3, 3)
    landed(piece(1, 1, k), ry.at[0, 1])
    to_partner(1, 1)
    stays.append(compute(3))
    stays.append(compute(1))
    landed(piece(2, 0, k), ry.at[1, 0])
    to_partner(2, 0)
    landed(piece(2, 2, k), ry.at[1, 2])
    to_partner(2, 2)
    landed(piece(2, 1, k), ry.at[1, 1])
    to_partner(2, 1)
    landed(piece(2, 3, k), ry.at[1, 3])
    to_partner(2, 3)
    stays.append(compute(2))
    for dh in (0, 3, 1, 2):
        for e in (1, 2, 3):
            landed(out.at[:, pl.ds(2 * ((x - e) % 4), 2), :, columns(dh)], ro.at[dh, e])
    for copy in pending:
        copy.wait_send()
    for stay in stays:
        stay.wait()
    pltpu.make_async_copy(count, count, s1).wait()


def main(raw, rims):
    vm = pl.BlockSpec(memory_space=pltpu.VMEM)
    anywhere = pl.BlockSpec(memory_space=pl.ANY)
    dma = pltpu.SemaphoreType.DMA
    bf16, f32 = jnp.bfloat16, jnp.float32
    return pl.pallas_call(
        main_kernel,
        out_shape=(
            jax.ShapeDtypeStruct((CD, 2 * WD, F), bf16),
            jax.ShapeDtypeStruct((2, 8, CD, 512), f32),
        ),
        in_specs=[anywhere] * 3,
        out_specs=(vm, anywhere),
        scratch_shapes=[
            pltpu.VMEM(raw.shape, bf16),
            pltpu.VMEM(rims.shape, bf16),
            pltpu.VMEM((2, 2 * F, KP), bf16),
            pltpu.VMEM((F, F), f32),
            pltpu.VMEM((768, 256), bf16),
            pltpu.VMEM((256, 256), bf16),
            pltpu.VMEM((NBLK + 2, CD, 256), bf16),
            pltpu.VMEM((CD, 17280), f32),
            pltpu.VMEM((CD * (WD + 1), KP), bf16),
            pltpu.VMEM((512, 128), f32),
            pltpu.VMEM((16, 4, 8, 128), bf16),
            pltpu.VMEM((2, 4, 8, 8, 128), bf16),
            pltpu.VMEM((PAIRS, 8, 128), bf16),
            pltpu.VMEM((4, 4, 2, CD, 1024), bf16),
            pltpu.VMEM((2, 2, 4, CD, 1024), bf16),
            pltpu.VMEM((4, 2, 2, 4, CD, 128), f32),
            dma((3,)),
            dma(()),
            dma(()),
            dma(()),
            dma((3, 4)),
            dma((3, 4)),
            dma((4, 4)),
            dma((4, 4)),
            dma((4, 4)),
            dma((4, 4)),
        ],
        compiler_params=pltpu.CompilerParams(
            vmem_limit_bytes=53504 * 1024, collective_id=0, has_side_effects=True
        ),
        name="main",
    )(raw, rims, build_table())


def on_device(raw):
    stored, totals = main(raw, exchange_rims(raw))
    return jnp.transpose(stored, (2, 0, 1)), totals * jnp.float32(1.0 / (16 * WD))


def solution(mesh):
    return jax.shard_map(
        on_device,
        mesh=mesh,
        in_specs=(P("chan", "tm"),),
        out_specs=(P(None, "chan", "tm"), P(None, "tm", "chan", None)),
        check_vma=False,
    )
```
